128 devices in a mesh: rows: 8 (over x, y_hi), cols: 16 (over z, y_lo, core).
Axes of the slice: x: 4, y: 4 (y_hi: 2, y_lo: 2; y = y_hi * 2 + y_lo), z: 4, core: 2. Of those that a mesh axis runs over, the one named last changes fastest.
Arguments:
- image: bfloat16 [256, 16384], P('rows', 'cols'), may hold values from -6 to 6
- w_in: float32 [64, 256], replicated, may hold values from -0.75 to 0.75
- conv_w: float32 [9, 128], replicated, may hold values from -2 to 2
- conv_b: float32 [128], replicated, may hold values from -3 to 3
- w_x: float32 [4, 128, 36], replicated, may hold values from -0.5 to 0.5
- w_dt: float32 [4, 4, 128], replicated, may hold values from -3 to 3
- dt_bias: float32 [4, 128], replicated, may hold values from -3 to -1
- a_log: float32 [4, 128, 16], replicated, may hold values from -7 to 0.7
- d_skip: float32 [4, 128], replicated, may hold values from -4 to 4
- ln_gain: float32 [128], replicated, may hold values from 0.5 to 1.5
- ln_bias: float32 [128], replicated, may hold values from -3 to 3
- w_out: float32 [128, 64], replicated, may hold values from -0.5 to 0.5
- cotangent: bfloat16 [256, 16384], P('rows', 'cols'), may hold values from -6 to 6
Outputs:
- output: bfloat16 [256, 16384], P('rows', 'cols')
- grad_image: bfloat16 [256, 16384], P('rows', 'cols')
- grad_w_in: float32 [64, 256], replicated
- grad_conv_w: float32 [9, 128], replicated
- grad_conv_b: float32 [128], replicated
- grad_w_x: float32 [4, 128, 36], replicated
- grad_w_dt: float32 [4, 4, 128], replicated
- grad_dt_bias: float32 [4, 128], replicated
- grad_a_log: float32 [4, 128, 16], replicated
- grad_d_skip: float32 [4, 128], replicated
- grad_ln_gain: float32 [128], replicated
- grad_ln_bias: float32 [128], replicated
- grad_w_out: float32 [128, 64], replicated
The draws below stay inside these ranges and needn't reach their ends.
All inputs are finite; a program needn't handle non-finite values.
Results may differ from the reference program's by a relative error of at most 0.0015.
Values sent between devices are 32-bit elements; how exact they have to be, the bound alone decides.
A program may use at most 320 MiB of HBM per device.

```python
import jax
import jax.numpy as jnp
from jax import lax

D = 64
E = 128
STATE = 16
RANK = 4
DIRS = 4
CHANNELS = 256
SAMPLES = 256


def levels(key, shape, cuts, smallest, top_value):
    def one(position, blocks):
        steps = jax.random.uniform(jax.random.fold_in(jax.random.fold_in(key, 6), position), (blocks,), jnp.float32, smallest / len(cuts), top_value / len(cuts))
        return jnp.repeat(jnp.exp(steps), shape[position] // blocks).reshape((-1,) + (1,) * (len(shape) - position - 1))

    loudness = one(*cuts[0])
    for cut in cuts[1:]:
        loudness = loudness * one(*cut)
    return loudness


def gaussian(key, extent, deviation, most, cuts=(), held_as=jnp.bfloat16):
    values = jax.random.normal(key, extent, jnp.float32) * deviation
    if len(cuts) > 0:
        values = levels(key, extent, cuts, -0.22, 0.18) * values
    return jnp.clip(values, min=-most, max=most).astype(held_as)


def setup_inputs(seed: int = 0) -> dict:
    keys = jax.random.split(jax.random.key(seed), 14)
    return {
        "image": gaussian(keys[0], (CHANNELS, SAMPLES * D), 1.0, 6.0, ((0, 8), (1, 16))),
        "w_in": gaussian(keys[1], (D, 2 * E), D ** -0.5, 0.75, (), jnp.float32),
        "conv_w": gaussian(keys[2], (9, E), 9 ** -0.5, 2.0, (), jnp.float32),
        "conv_b": gaussian(keys[3], (E,), 0.5, 3.0, (), jnp.float32),
        "w_x": gaussian(keys[4], (DIRS, E, RANK + 2 * STATE), E ** -0.5, 0.5, (), jnp.float32),
        "w_dt": gaussian(keys[5], (DIRS, RANK, E), RANK ** -0.5, 3.0, (), jnp.float32),
        "dt_bias": jnp.clip(jax.random.uniform(keys[6], (DIRS, E), jnp.float32, -3.0, -1.0), -3.0, -1.0),
        "a_log": jnp.clip(jax.random.uniform(keys[7], (DIRS, E, STATE), jnp.float32, -7.0, 0.7), -7.0, 0.7),
        "d_skip": gaussian(keys[8], (DIRS, E), 1.0, 4.0, (), jnp.float32),
        "ln_gain": jnp.clip(jax.random.uniform(keys[9], (E,), jnp.float32, 0.5, 1.5), 0.5, 1.5),
        "ln_bias": gaussian(keys[10], (E,), 0.5, 3.0, (), jnp.float32),
        "w_out": gaussian(keys[11], (E, D), E ** -0.5, 0.5, (), jnp.float32),
        "cotangent": gaussian(keys[12], (CHANNELS, SAMPLES * D), 1.0, 6.0, ((0, 8), (1, 16))),
    }


EXACT_MATH_MODE = lax.Precision.HIGHEST

def project_in(pixels, w_in):
    mixed = jnp.einsum('rcd,de->rce', pixels.astype(jnp.float32), w_in, precision=EXACT_MATH_MODE)
    halfway = w_in.shape[1] // 2
    return (mixed[:, :, :halfway], mixed[:, :, halfway:])

def convolve(padded, conv_w, conv_b):
    height = padded.shape[0] - 2
    breadth = padded.shape[1] - 2
    running = conv_b + conv_w[0] * padded[0:height, 0:breadth]
    for tap in range(1, 9):
        running = running + conv_w[tap] * padded[tap // 3:tap // 3 + height, tap % 3:tap % 3 + breadth]
    return running

def activate(conv_out):
    return jax.nn.silu(conv_out)

def prepare(activated, w_proj, w_step, step_bias, log_rate):
    width_rank = w_step.shape[0]
    state_width = log_rate.shape[1]
    projected = jnp.einsum('rce,ef->rcf', activated, w_proj, precision=EXACT_MATH_MODE)
    step_size = jax.nn.softplus(jnp.einsum('rcq,qe->rce', projected[:, :, :width_rank], w_step, precision=EXACT_MATH_MODE) + step_bias)
    b_in = projected[:, :, width_rank:width_rank + state_width]
    c_out = projected[:, :, width_rank + state_width:]
    return (step_size, b_in, c_out, -jnp.exp(log_rate))

def run_scan(h_start, activated, step_size, b_in, c_out, decay_rate, skip_weight_factor):

    def advance(hidden_state, inputs):
        input_at_step, d_t, b_t, readout_at_step = inputs
        factor = jnp.exp(d_t[:, :, None] * decay_rate)
        hidden_state = factor * hidden_state + (d_t * input_at_step)[:, :, None] * b_t[:, None, :]
        final_answer = jnp.einsum('sen,sn->se', hidden_state, readout_at_step, precision=EXACT_MATH_MODE) + skip_weight_factor * input_at_step
        return (hidden_state, final_answer)
    h_last, outputs = lax.scan(advance, h_start, (activated, step_size, b_in, c_out))
    return (outputs, h_last)

def arrange(values, k):
    if k < 2:
        values = jnp.swapaxes(values, 0, 1)
    if k % 2 == 1:
        values = jnp.flip(values, 0)
    return values

def restore(values, k):
    if k % 2 == 1:
        values = jnp.flip(values, 0)
    if k < 2:
        values = jnp.swapaxes(values, 0, 1)
    return values

def finish(summed, gate_in, ln_gain, ln_bias, w_out):
    average = lax.optimization_barrier(jnp.mean(summed, axis=2, keepdims=True))
    centred = summed - average
    spread = lax.optimization_barrier(jnp.mean(centred * centred, axis=2, keepdims=True))
    normed = centred * lax.rsqrt(spread + 1e-05) * ln_gain + ln_bias
    gated = normed * jax.nn.silu(gate_in)
    return jnp.einsum('rce,ed->rcd', gated, w_out, precision=EXACT_MATH_MODE).astype(jnp.bfloat16)

def scan_grads(ordered, decay_rate, skip_weight_factor, output_gradient):
    length = ordered[0].shape[0]
    lines = ordered[0].shape[1]
    groups = lines // 8

    def split(values):
        return jnp.swapaxes(values.reshape((length, groups, 8) + values.shape[2:]), 0, 1)

    def one_group(pieces):
        h_start = jnp.zeros((8, decay_rate.shape[0], decay_rate.shape[1]), jnp.float32)

        def forward(act_in, step_in, b_part, readout_piece, rate_in, skip_in):
            return run_scan(h_start, act_in, step_in, b_part, readout_piece, rate_in, skip_in)
        _, backward = jax.vjp(forward, pieces[0], pieces[1], pieces[2], pieces[3], decay_rate, skip_weight_factor)
        return backward((pieces[4], jnp.zeros_like(h_start)))
    results = lax.map(one_group, (split(ordered[0]), split(ordered[1]), split(ordered[2]), split(ordered[3]), split(output_gradient)))

    def join(values):
        return jnp.swapaxes(values, 0, 1).reshape((length, lines) + values.shape[3:])
    return (join(results[0]), join(results[1]), join(results[2]), join(results[3]), lax.optimization_barrier(jnp.sum(results[4], axis=0)), lax.optimization_barrier(jnp.sum(results[5], axis=0)))

def reference(image, w_in, conv_w, conv_b, w_x, w_dt, dt_bias, a_log, d_skip, ln_gain, ln_bias, w_out, cotangent):
    width = w_in.shape[0]
    pixels = image.reshape(image.shape[0], image.shape[1] // width, width)
    (inner_in, gate_in), in_back = jax.vjp(project_in, pixels, w_in)
    padded = jnp.pad(inner_in, ((1, 1), (1, 1), (0, 0)))
    conv_out, conv_back = jax.vjp(convolve, padded, conv_w, conv_b)
    activated, act_back = jax.vjp(activate, conv_out)
    summed = jnp.zeros_like(activated)
    saved = []
    for k in range(4):
        prepared, prep_back = jax.vjp(prepare, activated, w_x[k], w_dt[k], dt_bias[k], a_log[k])
        step_size, b_in, c_out, decay_rate = prepared
        ordered = (arrange(activated, k), arrange(step_size, k), arrange(b_in, k), arrange(c_out, k))
        h_start = jnp.zeros((ordered[0].shape[1], decay_rate.shape[0], decay_rate.shape[1]), jnp.float32)
        outputs, _ = run_scan(h_start, ordered[0], ordered[1], ordered[2], ordered[3], decay_rate, d_skip[k])
        summed = summed + restore(outputs, k)
        saved.append((ordered, decay_rate, prep_back))
    output, fin_back = jax.vjp(finish, summed, gate_in, ln_gain, ln_bias, w_out)
    g_sum, g_gate, g_gain, g_lnb, g_wout = fin_back(cotangent.reshape(output.shape))
    g_u = jnp.zeros_like(activated)
    g_wx, g_wdt, g_bias, g_alog, g_skip = ([], [], [], [], [])
    for k in range(4):
        ordered, decay_rate, prep_back = saved[k]
        gradients = scan_grads(ordered, decay_rate, d_skip[k], arrange(g_sum, k))
        g_prep = prep_back((restore(gradients[1], k), restore(gradients[2], k), restore(gradients[3], k), gradients[4]))
        g_u = g_u + restore(gradients[0], k) + g_prep[0]
        g_wx.append(g_prep[1])
        g_wdt.append(g_prep[2])
        g_bias.append(g_prep[3])
        g_alog.append(g_prep[4])
        g_skip.append(gradients[5])
    g_conv = act_back(g_u)[0]
    g_pad, g_cw, g_cb = conv_back(g_conv)
    g_x, g_win = in_back((g_pad[1:-1, 1:-1], g_gate))
    return (output.reshape(image.shape), g_x.reshape(image.shape), g_win, g_cw, g_cb, jnp.stack(g_wx), jnp.stack(g_wdt), jnp.stack(g_bias), jnp.stack(g_alog), jnp.stack(g_skip), g_gain, g_lnb, g_wout)
```

```python
import jax
import jax.numpy as jnp
from jax import lax
from jax.sharding import PartitionSpec as P

EXACT_MATH_MODE = lax.Precision.HIGHEST


def entering(part, axis, flips):
    count = lax.axis_size(axis)
    place = lax.axis_index(axis)
    gathered = lax.all_gather(jnp.stack(part), axis)
    per = part[0].shape[0] // len(flips)
    states = []
    for group, reverse in enumerate(flips):
        ahead = count - 1 - place if reverse else place
        piece = gathered[:, :, group * per : (group + 1) * per]
        state = (jnp.ones_like(piece[0, 0]), jnp.zeros_like(piece[0, 1]))
        for lap in range(count - 1):
            source = count - 1 - lap if reverse else lap
            fresh = combine(state, (piece[source, 0], piece[source, 1]))
            state = jax.tree.map(lambda n, o: jnp.where(lap < ahead, n, o), fresh, state)
        states.append(state[1])
    return jnp.concatenate(states, axis=0)


def extended(array, sides, width):
    for axis, dim in sides:
        devices, length = (lax.axis_size(axis), array.shape[dim])
        up = [(i, (i + 1) % devices) for i in range(devices - 1)]
        down = [(j, i) for i, j in up]
        last = lax.slice_in_dim(array, length - width, length, axis=dim)
        leading = lax.slice_in_dim(array, 0, width, axis=dim)
        before = lax.ppermute(last, axis, up)
        after = lax.ppermute(leading, axis, down)
        array = jnp.concatenate([before, array, after], axis=dim)
    return array


def project_in(pixels, w_in):
    mixed = jnp.einsum("rcd,de->rce", pixels.astype(jnp.float32), w_in, precision=EXACT_MATH_MODE)
    halfway = w_in.shape[1] // 2
    return (mixed[:, :, :halfway], mixed[:, :, halfway:])


def convolve(padded, conv_w, conv_b):
    height = padded.shape[0] - 2
    breadth = padded.shape[1] - 2
    running = conv_b + conv_w[0] * padded[0:height, 0:breadth]
    for tap in range(1, 9):
        running = (
            running
            + conv_w[tap] * padded[tap // 3 : tap // 3 + height, tap % 3 : tap % 3 + breadth]
        )
    return running


def activate(conv_out):
    return jax.nn.silu(conv_out)


def prepare(activated, w_proj, w_step, step_bias, log_rate):
    width_rank = w_step.shape[0]
    state_width = log_rate.shape[1]
    projected = jnp.einsum("rce,ef->rcf", activated, w_proj, precision=EXACT_MATH_MODE)
    step_size = jax.nn.softplus(
        jnp.einsum("rcq,qe->rce", projected[:, :, :width_rank], w_step, precision=EXACT_MATH_MODE)
        + step_bias
    )
    b_in = projected[:, :, width_rank : width_rank + state_width]
    c_out = projected[:, :, width_rank + state_width :]
    return (step_size, b_in, c_out, -jnp.exp(log_rate))


def run_scan(h_start, activated, step_size, b_in, c_out, rate_lines, skip_lines):
    def advance(hidden_state, inputs):
        input_at_step, d_t, b_t, readout_at_step = inputs
        factor = jnp.exp(d_t[:, None, :] * rate_lines)
        hidden_state = factor * hidden_state + (d_t * input_at_step)[:, None, :] * b_t[:, :, None]
        final_answer = (
            jnp.einsum("qcw,qc->qw", hidden_state, readout_at_step, precision=EXACT_MATH_MODE)
            + skip_lines * input_at_step
        )
        return (hidden_state, final_answer)

    h_last, outputs = lax.scan(advance, h_start, (activated, step_size, b_in, c_out), unroll=8)
    return (outputs, h_last)


def cumulative_decay(step_size, rate_lines):
    return jnp.exp(jnp.cumsum(step_size, axis=0)[:, :, None, :] * rate_lines[None])


def arrange(values, k):
    if k < 2:
        values = jnp.swapaxes(values, 0, 1)
    if k % 2 == 1:
        values = jnp.flip(values, 0)
    return values


def restore(values, k):
    if k % 2 == 1:
        values = jnp.flip(values, 0)
    if k < 2:
        values = jnp.swapaxes(values, 0, 1)
    return values


def finish(summed, gate_in, ln_gain, ln_bias, w_out):
    average = jnp.mean(summed, axis=2, keepdims=True)
    centred = summed - average
    spread = jnp.mean(centred * centred, axis=2, keepdims=True)
    normed = centred * lax.rsqrt(spread + 1e-05) * ln_gain + ln_bias
    gated = normed * jax.nn.silu(gate_in)
    return jnp.einsum("rce,ed->rcd", gated, w_out, precision=EXACT_MATH_MODE).astype(jnp.bfloat16)


def combine(earlier, later):
    return (earlier[0] * later[0], later[1] + later[0] * earlier[1])


def joined(values, ks):
    return jnp.concatenate([arrange(v, k) for v, k in zip(values, ks)], axis=1)


def parted(values, ks):
    return [restore(v, k) for v, k in zip(jnp.split(values, len(ks), axis=1), ks)]


def chain_forward(ks, activated, prepared, d_skip):
    ordered = (
        joined([activated] * len(ks), ks),
        joined([p[0] for p in prepared], ks),
        joined([p[1] for p in prepared], ks),
        joined([p[2] for p in prepared], ks),
    )
    rates = jnp.stack([p[3] for p in prepared])
    skips = jnp.stack([d_skip[k] for k in ks])
    per = ordered[0].shape[1] // len(ks)
    axis = "cols" if ks[0] < 2 else "rows"

    def rate_of(rates):
        return jnp.repeat(jnp.swapaxes(rates, 1, 2), per, axis=0)

    h_zero = jnp.zeros((ordered[0].shape[1], rates.shape[2], rates.shape[1]), jnp.float32)

    def local_scan(act_in, step_in, b_part, readout_piece, rate_in, skip_in):
        return run_scan(
            h_zero, act_in, step_in, b_part, readout_piece, rate_of(rate_in),
            jnp.repeat(skip_in, per, axis=0),
        )

    (out_local, h_local), local_back = jax.vjp(
        local_scan, ordered[0], ordered[1], ordered[2], ordered[3], rates, skips
    )
    decay_factors, decay_back = jax.vjp(
        lambda s, r: cumulative_decay(s, rate_of(r)), ordered[1], rates
    )
    fading = decay_factors[-1]
    h_start = entering((fading, h_local), axis, [k % 2 == 1 for k in ks])

    def carried(decay_in, readout_piece):
        extra = jnp.einsum(
            "lsne,lsn->lse", decay_in * h_start, readout_piece, precision=EXACT_MATH_MODE
        )
        return (extra, decay_in[-1] * h_start)

    (extra, _), carry_back = jax.vjp(carried, decay_factors, ordered[3])
    return (
        parted(out_local + extra, ks),
        (local_back, decay_back, carry_back, decay_factors, ordered[3]),
    )


def chain_backward(ks, memory, g_sum):
    local_back, decay_back, carry_back, decay_factors, readout_piece = memory
    axis = "cols" if ks[0] < 2 else "rows"
    output_gradient = joined([g_sum] * len(ks), ks)
    partial_total = jnp.einsum(
        "dwq,dwy,dwyq->wyq",
        output_gradient,
        readout_piece,
        decay_factors,
        precision=EXACT_MATH_MODE,
    )
    g_last = entering((decay_factors[-1], partial_total), axis, [k % 2 == 0 for k in ks])
    g_local = local_back((output_gradient, g_last))
    g_decay, g_c_carry = carry_back((output_gradient, g_last))
    g_step_carry, g_rate_carry = decay_back(g_decay)
    g_rate = g_local[4] + g_rate_carry
    return [
        (u, s, b, c, g_rate[i], g_local[5][i])
        for i, (u, s, b, c) in enumerate(
            zip(
                parted(g_local[0], ks),
                parted(g_local[1] + g_step_carry, ks),
                parted(g_local[2], ks),
                parted(g_local[3] + g_c_carry, ks),
            )
        )
    ]


PAIRS = ((0, 1), (2, 3))


def body(
    image,
    w_in,
    conv_w,
    conv_b,
    w_x,
    w_dt,
    dt_bias,
    a_log,
    d_skip,
    ln_gain,
    ln_bias,
    w_out,
    cotangent,
):
    width = w_in.shape[0]
    pixels = image.reshape(image.shape[0], image.shape[1] // width, width)
    (inner_in, gate_in), in_back = jax.vjp(project_in, pixels, w_in)
    padded = extended(inner_in, (("rows", 0), ("cols", 1)), 1)

    def conv_weights(taps, offsets):
        return convolve(padded, taps, offsets)

    conv_out, conv_back = jax.vjp(conv_weights, conv_w, conv_b)
    activated, act_back = jax.vjp(activate, conv_out)
    prepared_all = []
    prep_backs = []
    for k in range(4):
        prepared, prep_back = jax.vjp(prepare, activated, w_x[k], w_dt[k], dt_bias[k], a_log[k])
        prepared_all.append(prepared)
        prep_backs.append(prep_back)
    summed = jnp.zeros_like(activated)
    memories = []
    for ks in PAIRS:
        outputs, memory = chain_forward(ks, activated, [prepared_all[k] for k in ks], d_skip)
        for piece in outputs:
            summed = summed + piece
        memories.append(memory)
    output, fin_back = jax.vjp(finish, summed, gate_in, ln_gain, ln_bias, w_out)
    g_sum, g_gate, g_gain, g_lnb, g_wout = fin_back(cotangent.reshape(output.shape))
    g_u = jnp.zeros_like(activated)
    per_k = [None] * 4
    for ks, memory in zip(PAIRS, memories):
        for k, gradients in zip(ks, chain_backward(ks, memory, g_sum)):
            g_u = g_u + gradients[0]
            per_k[k] = gradients[1:]
    g_wx, g_wdt, g_bias, g_alog, g_skip = ([], [], [], [], [])
    for k in range(4):
        g_step, g_b, g_c, g_rate, g_skip_k = per_k[k]
        g_prep = prep_backs[k]((g_step, g_b, g_c, g_rate))
        g_u = g_u + g_prep[0]
        g_wx.append(g_prep[1])
        g_wdt.append(g_prep[2])
        g_bias.append(g_prep[3])
        g_alog.append(g_prep[4])
        g_skip.append(g_skip_k)
    g_conv = act_back(g_u)[0]
    g_cw, g_cb = conv_back(g_conv)
    g_pad = extended(g_conv, (("rows", 0), ("cols", 1)), 1)
    height = g_conv.shape[0]
    breadth = g_conv.shape[1]
    g_inner = conv_w[0] * g_pad[2 : 2 + height, 2 : 2 + breadth]
    for tap in range(1, 9):
        row_off = 2 - tap // 3
        col_off = 2 - tap % 3
        g_inner = (
            g_inner + conv_w[tap] * g_pad[row_off : row_off + height, col_off : col_off + breadth]
        )
    g_x, g_win = in_back((g_inner, g_gate))
    pieces = (
        g_win,
        g_cw,
        g_cb,
        jnp.stack(g_wx),
        jnp.stack(g_wdt),
        jnp.stack(g_bias),
        jnp.stack(g_alog),
        jnp.stack(g_skip),
        g_gain,
        g_lnb,
        g_wout,
    )
    flat = lax.psum(jnp.concatenate([p.reshape(-1) for p in pieces]), ("rows", "cols"))
    totals = []
    offset = 0
    for p in pieces:
        totals.append(flat[offset : offset + p.size].reshape(p.shape))
        offset += p.size
    return (
        output.reshape(image.shape),
        g_x.reshape(image.shape),
        totals[0],
        totals[1],
        totals[2],
        totals[3],
        totals[4],
        totals[5],
        totals[6],
        totals[7],
        totals[8],
        totals[9],
        totals[10],
    )


def solution(mesh):
    in_specs = (
        P("rows", "cols"),
        P(),
        P(),
        P(),
        P(),
        P(),
        P(),
        P(),
        P(),
        P(),
        P(),
        P(),
        P("rows", "cols"),
    )
    out_specs = (
        P("rows", "cols"),
        P("rows", "cols"),
        P(),
        P(),
        P(),
        P(),
        P(),
        P(),
        P(),
        P(),
        P(),
        P(),
        P(),
    )
    return jax.shard_map(body, mesh=mesh, in_specs=in_specs, out_specs=out_specs, check_vma=False)
```

```python
import jax
import jax.numpy as jnp
from jax import lax
from jax.sharding import PartitionSpec as P

EXACT_MATH_MODE = lax.Precision.HIGHEST


def entering(part, axis, flips):
    count = lax.axis_size(axis)
    place = lax.axis_index(axis)
    gathered = lax.all_gather(jnp.stack(part), axis)
    per = part[0].shape[0] // len(flips)
    states = []
    for group, reverse in enumerate(flips):
        ahead = count - 1 - place if reverse else place
        piece = gathered[:, :, group * per : (group + 1) * per]
        state = (jnp.ones_like(piece[0, 0]), jnp.zeros_like(piece[0, 1]))
        for lap in range(count - 1):
            source = count - 1 - lap if reverse else lap
            fresh = combine(state, (piece[source, 0], piece[source, 1]))
            state = jax.tree.map(lambda n, o: jnp.where(lap < ahead, n, o), fresh, state)
        states.append(state[1])
    return jnp.concatenate(states, axis=0)


def extended(array, sides, width):
    for axis, dim in sides:
        devices, length = (lax.axis_size(axis), array.shape[dim])
        up = [(i, (i + 1) % devices) for i in range(devices - 1)]
        down = [(j, i) for i, j in up]
        last = lax.slice_in_dim(array, length - width, length, axis=dim)
        leading = lax.slice_in_dim(array, 0, width, axis=dim)
        before = lax.ppermute(last, axis, up)
        after = lax.ppermute(leading, axis, down)
        array = jnp.concatenate([before, array, after], axis=dim)
    return array


def project_in(pixels, w_in):
    mixed = jnp.einsum("rcd,de->rce", pixels.astype(jnp.float32), w_in, precision=EXACT_MATH_MODE)
    halfway = w_in.shape[1] // 2
    return (mixed[:, :, :halfway], mixed[:, :, halfway:])


def convolve(padded, conv_w, conv_b):
    height = padded.shape[0] - 2
    breadth = padded.shape[1] - 2
    running = conv_b + conv_w[0] * padded[0:height, 0:breadth]
    for tap in range(1, 9):
        running = (
            running
            + conv_w[tap] * padded[tap // 3 : tap // 3 + height, tap % 3 : tap % 3 + breadth]
        )
    return running


def activate(conv_out):
    return jax.nn.silu(conv_out)


def prepare(activated, w_proj, w_step, step_bias, log_rate):
    width_rank = w_step.shape[0]
    state_width = log_rate.shape[1]
    projected = jnp.einsum("rce,ef->rcf", activated, w_proj, precision=EXACT_MATH_MODE)
    step_size = jax.nn.softplus(
        jnp.einsum("rcq,qe->rce", projected[:, :, :width_rank], w_step, precision=EXACT_MATH_MODE)
        + step_bias
    )
    b_in = projected[:, :, width_rank : width_rank + state_width]
    c_out = projected[:, :, width_rank + state_width :]
    return (step_size, b_in, c_out, -jnp.exp(log_rate))


def run_scan(h_start, activated, step_size, b_in, c_out, rate_lines, skip_lines):
    def advance(hidden_state, inputs):
        input_at_step, d_t, b_t, readout_at_step = inputs
        factor = jnp.exp(d_t[:, None, :] * rate_lines)
        hidden_state = factor * hidden_state + (d_t * input_at_step)[:, None, :] * b_t[:, :, None]
        final_answer = (
            jnp.einsum("qcw,qc->qw", hidden_state, readout_at_step, precision=EXACT_MATH_MODE)
            + skip_lines * input_at_step
        )
        return (hidden_state, final_answer)

    h_last, outputs = lax.scan(advance, h_start, (activated, step_size, b_in, c_out), unroll=8)
    return (outputs, h_last)


def cumulative_decay(step_size, rate_lines):
    return jnp.exp(jnp.cumsum(step_size, axis=0)[:, :, None, :] * rate_lines[None])


def arrange(values, k):
    if k < 2:
        values = jnp.swapaxes(values, 0, 1)
    if k % 2 == 1:
        values = jnp.flip(values, 0)
    return values


def restore(values, k):
    if k % 2 == 1:
        values = jnp.flip(values, 0)
    if k < 2:
        values = jnp.swapaxes(values, 0, 1)
    return values


def finish(summed, gate_in, ln_gain, ln_bias, w_out):
    average = jnp.mean(summed, axis=2, keepdims=True)
    centred = summed - average
    spread = jnp.mean(centred * centred, axis=2, keepdims=True)
    normed = centred * lax.rsqrt(spread + 1e-05) * ln_gain + ln_bias
    gated = normed * jax.nn.silu(gate_in)
    return jnp.einsum("rce,ed->rcd", gated, w_out, precision=EXACT_MATH_MODE).astype(jnp.bfloat16)


def combine(earlier, later):
    return (earlier[0] * later[0], later[1] + later[0] * earlier[1])


def joined(values, ks):
    return jnp.concatenate([arrange(v, k) for v, k in zip(values, ks)], axis=1)


def parted(values, ks):
    return [restore(v, k) for v, k in zip(jnp.split(values, len(ks), axis=1), ks)]


def chain_forward(ks, activated, prepared, d_skip):
    ordered = (
        joined([activated] * len(ks), ks),
        joined([p[0] for p in prepared], ks),
        joined([p[1] for p in prepared], ks),
        joined([p[2] for p in prepared], ks),
    )
    rates = jnp.stack([p[3] for p in prepared])
    skips = jnp.stack([d_skip[k] for k in ks])
    per = ordered[0].shape[1] // len(ks)
    axis = "cols" if ks[0] < 2 else "rows"

    def rate_of(rates):
        return jnp.repeat(jnp.swapaxes(rates, 1, 2), per, axis=0)

    h_zero = jnp.zeros((ordered[0].shape[1], rates.shape[2], rates.shape[1]), jnp.float32)

    def local_scan(act_in, step_in, b_part, readout_piece, rate_in, skip_in):
        return run_scan(
            h_zero, act_in, step_in, b_part, readout_piece, rate_of(rate_in),
            jnp.repeat(skip_in, per, axis=0),
        )

    (out_local, h_local), local_back = jax.vjp(
        local_scan, ordered[0], ordered[1], ordered[2], ordered[3], rates, skips
    )
    decay_factors, decay_back = jax.vjp(
        lambda s, r: cumulative_decay(s, rate_of(r)), ordered[1], rates
    )
    fading = decay_factors[-1]
    h_start = entering((fading, h_local), axis, [k % 2 == 1 for k in ks])

    def carried(decay_in, readout_piece):
        extra = jnp.einsum(
            "lsne,lsn->lse", decay_in * h_start, readout_piece, precision=EXACT_MATH_MODE
        )
        return (extra, decay_in[-1] * h_start)

    (extra, _), carry_back = jax.vjp(carried, decay_factors, ordered[3])
    return (
        parted(out_local + extra, ks),
        (local_back, decay_back, carry_back, decay_factors, ordered[3]),
    )


def chain_backward(ks, memory, g_sum):
    local_back, decay_back, carry_back, decay_factors, readout_piece = memory
    axis = "cols" if ks[0] < 2 else "rows"
    output_gradient = joined([g_sum] * len(ks), ks)
    partial_total = jnp.einsum(
        "dwq,dwy,dwyq->wyq",
        output_gradient,
        readout_piece,
        decay_factors,
        precision=EXACT_MATH_MODE,
    )
    g_last = entering((decay_factors[-1], partial_total), axis, [k % 2 == 0 for k in ks])
    g_local = local_back((output_gradient, g_last))
    g_decay, g_c_carry = carry_back((output_gradient, g_last))
    g_step_carry, g_rate_carry = decay_back(g_decay)
    g_rate = g_local[4] + g_rate_carry
    return [
        (u, s, b, c, g_rate[i], g_local[5][i])
        for i, (u, s, b, c) in enumerate(
            zip(
                parted(g_local[0], ks),
                parted(g_local[1] + g_step_carry, ks),
                parted(g_local[2], ks),
                parted(g_local[3] + g_c_carry, ks),
            )
        )
    ]


def summed_everywhere(flat, axes):
    for axis in axes:
        devices = lax.axis_size(axis)
        if devices & (devices - 1):
            flat = lax.psum(flat, axis)
            continue
        stride = 1
        while stride < devices:
            flat = flat + lax.ppermute(flat, axis, [(i, i ^ stride) for i in range(devices)])
            stride *= 2
    return flat


PAIRS = ((0, 1), (2, 3))


def body(
    image,
    w_in,
    conv_w,
    conv_b,
    w_x,
    w_dt,
    dt_bias,
    a_log,
    d_skip,
    ln_gain,
    ln_bias,
    w_out,
    cotangent,
):
    width = w_in.shape[0]
    pixels = image.reshape(image.shape[0], image.shape[1] // width, width)
    (inner_in, gate_in), in_back = jax.vjp(project_in, pixels, w_in)
    padded = extended(inner_in, (("rows", 0), ("cols", 1)), 1)

    def conv_weights(taps, offsets):
        return convolve(padded, taps, offsets)

    conv_out, conv_back = jax.vjp(conv_weights, conv_w, conv_b)
    activated, act_back = jax.vjp(activate, conv_out)
    prepared_all = []
    prep_backs = []
    for k in range(4):
        prepared, prep_back = jax.vjp(prepare, activated, w_x[k], w_dt[k], dt_bias[k], a_log[k])
        prepared_all.append(prepared)
        prep_backs.append(prep_back)
    summed = jnp.zeros_like(activated)
    memories = []
    for ks in PAIRS:
        outputs, memory = chain_forward(ks, activated, [prepared_all[k] for k in ks], d_skip)
        for piece in outputs:
            summed = summed + piece
        memories.append(memory)
    output, fin_back = jax.vjp(finish, summed, gate_in, ln_gain, ln_bias, w_out)
    g_sum, g_gate, g_gain, g_lnb, g_wout = fin_back(cotangent.reshape(output.shape))
    g_u = jnp.zeros_like(activated)
    per_k = [None] * 4
    for ks, memory in zip(PAIRS, memories):
        for k, gradients in zip(ks, chain_backward(ks, memory, g_sum)):
            g_u = g_u + gradients[0]
            per_k[k] = gradients[1:]
    g_wx, g_wdt, g_bias, g_alog, g_skip = ([], [], [], [], [])
    for k in range(4):
        g_step, g_b, g_c, g_rate, g_skip_k = per_k[k]
        g_prep = prep_backs[k]((g_step, g_b, g_c, g_rate))
        g_u = g_u + g_prep[0]
        g_wx.append(g_prep[1])
        g_wdt.append(g_prep[2])
        g_bias.append(g_prep[3])
        g_alog.append(g_prep[4])
        g_skip.append(g_skip_k)
    g_conv = act_back(g_u)[0]
    g_cw, g_cb = conv_back(g_conv)
    g_pad = extended(g_conv, (("rows", 0), ("cols", 1)), 1)
    height = g_conv.shape[0]
    breadth = g_conv.shape[1]
    g_inner = conv_w[0] * g_pad[2 : 2 + height, 2 : 2 + breadth]
    for tap in range(1, 9):
        row_off = 2 - tap // 3
        col_off = 2 - tap % 3
        g_inner = (
            g_inner + conv_w[tap] * g_pad[row_off : row_off + height, col_off : col_off + breadth]
        )
    g_x, g_win = in_back((g_inner, g_gate))
    pieces = (
        g_win,
        g_cw,
        g_cb,
        jnp.stack(g_wx),
        jnp.stack(g_wdt),
        jnp.stack(g_bias),
        jnp.stack(g_alog),
        jnp.stack(g_skip),
        g_gain,
        g_lnb,
        g_wout,
    )
    flat = summed_everywhere(jnp.concatenate([p.reshape(-1) for p in pieces]), ("cols", "rows"))
    totals = []
    offset = 0
    for p in pieces:
        totals.append(flat[offset : offset + p.size].reshape(p.shape))
        offset += p.size
    return (
        output.reshape(image.shape),
        g_x.reshape(image.shape),
        totals[0],
        totals[1],
        totals[2],
        totals[3],
        totals[4],
        totals[5],
        totals[6],
        totals[7],
        totals[8],
        totals[9],
        totals[10],
    )


def solution(mesh):
    in_specs = (
        P("rows", "cols"),
        P(),
        P(),
        P(),
        P(),
        P(),
        P(),
        P(),
        P(),
        P(),
        P(),
        P(),
        P("rows", "cols"),
    )
    out_specs = (
        P("rows", "cols"),
        P("rows", "cols"),
        P(),
        P(),
        P(),
        P(),
        P(),
        P(),
        P(),
        P(),
        P(),
        P(),
        P(),
    )
    return jax.shard_map(body, mesh=mesh, in_specs=in_specs, out_specs=out_specs, check_vma=False)
```

```python
import jax
import jax.numpy as jnp
from jax import lax
from jax.sharding import PartitionSpec as P

EXACT_MATH_MODE = lax.Precision.HIGHEST


def entering(sums, part, rate_lines, axis, flips):
    count = lax.axis_size(axis)
    place = lax.axis_index(axis)
    gathered = lax.all_gather(jnp.concatenate([sums[:, None, :], part], axis=1), axis)
    per = part.shape[0] // len(flips)
    states = []
    for group, reverse in enumerate(flips):
        ahead = count - 1 - place if reverse else place
        piece = gathered[:, group * per : (group + 1) * per]
        rate = rate_lines[group * per : (group + 1) * per]
        state = (jnp.ones_like(piece[0, :, 1:]), jnp.zeros_like(piece[0, :, 1:]))
        for lap in range(count - 1):
            source = count - 1 - lap if reverse else lap
            fading = jnp.exp(piece[source, :, :1] * rate)
            fresh = combine(state, (fading, piece[source, :, 1:]))
            state = jax.tree.map(lambda n, o: jnp.where(lap < ahead, n, o), fresh, state)
        states.append(state[1])
    return jnp.concatenate(states, axis=0)


def extended(array, sides, width):
    for axis, dim in sides:
        devices, length = (lax.axis_size(axis), array.shape[dim])
        up = [(i, (i + 1) % devices) for i in range(devices - 1)]
        down = [(j, i) for i, j in up]
        last = lax.slice_in_dim(array, length - width, length, axis=dim)
        leading = lax.slice_in_dim(array, 0, width, axis=dim)
        before = lax.ppermute(last, axis, up)
        after = lax.ppermute(leading, axis, down)
        array = jnp.concatenate([before, array, after], axis=dim)
    return array


def project_in(pixels, w_in):
    mixed = jnp.einsum("rcd,de->rce", pixels.astype(jnp.float32), w_in, precision=EXACT_MATH_MODE)
    halfway = w_in.shape[1] // 2
    return (mixed[:, :, :halfway], mixed[:, :, halfway:])


def convolve(padded, conv_w, conv_b):
    height = padded.shape[0] - 2
    breadth = padded.shape[1] - 2
    running = conv_b + conv_w[0] * padded[0:height, 0:breadth]
    for tap in range(1, 9):
        running = (
            running
            + conv_w[tap] * padded[tap // 3 : tap // 3 + height, tap % 3 : tap % 3 + breadth]
        )
    return running


def activate(conv_out):
    return jax.nn.silu(conv_out)


def prepare(activated, w_proj, w_step, step_bias, log_rate):
    width_rank = w_step.shape[0]
    state_width = log_rate.shape[1]
    projected = jnp.einsum("rce,ef->rcf", activated, w_proj, precision=EXACT_MATH_MODE)
    step_size = jax.nn.softplus(
        jnp.einsum("rcq,qe->rce", projected[:, :, :width_rank], w_step, precision=EXACT_MATH_MODE)
        + step_bias
    )
    b_in = projected[:, :, width_rank : width_rank + state_width]
    c_out = projected[:, :, width_rank + state_width :]
    return (step_size, b_in, c_out, -jnp.exp(log_rate))


def run_scan(h_start, activated, step_size, b_in, c_out, rate_lines, skip_lines):
    def advance(hidden_state, inputs):
        input_at_step, d_t, b_t, readout_at_step = inputs
        factor = jnp.exp(d_t[:, None, :] * rate_lines)
        hidden_state = factor * hidden_state + (d_t * input_at_step)[:, None, :] * b_t[:, :, None]
        final_answer = (
            jnp.einsum("qcw,qc->qw", hidden_state, readout_at_step, precision=EXACT_MATH_MODE)
            + skip_lines * input_at_step
        )
        return (hidden_state, final_answer)

    h_last, outputs = lax.scan(advance, h_start, (activated, step_size, b_in, c_out), unroll=8)
    return (outputs, h_last)


def cumulative_decay(step_size, rate_lines):
    return jnp.exp(jnp.cumsum(step_size, axis=0)[:, :, None, :] * rate_lines[None])


def arrange(values, k):
    if k < 2:
        values = jnp.swapaxes(values, 0, 1)
    if k % 2 == 1:
        values = jnp.flip(values, 0)
    return values


def restore(values, k):
    if k % 2 == 1:
        values = jnp.flip(values, 0)
    if k < 2:
        values = jnp.swapaxes(values, 0, 1)
    return values


def finish(summed, gate_in, ln_gain, ln_bias, w_out):
    average = jnp.mean(summed, axis=2, keepdims=True)
    centred = summed - average
    spread = jnp.mean(centred * centred, axis=2, keepdims=True)
    normed = centred * lax.rsqrt(spread + 1e-05) * ln_gain + ln_bias
    gated = normed * jax.nn.silu(gate_in)
    return jnp.einsum("rce,ed->rcd", gated, w_out, precision=EXACT_MATH_MODE).astype(jnp.bfloat16)


def combine(earlier, later):
    return (earlier[0] * later[0], later[1] + later[0] * earlier[1])


def joined(values, ks):
    return jnp.concatenate([arrange(v, k) for v, k in zip(values, ks)], axis=1)


def parted(values, ks):
    return [restore(v, k) for v, k in zip(jnp.split(values, len(ks), axis=1), ks)]


def chain_forward(ks, activated, prepared, d_skip):
    ordered = (
        joined([activated] * len(ks), ks),
        joined([p[0] for p in prepared], ks),
        joined([p[1] for p in prepared], ks),
        joined([p[2] for p in prepared], ks),
    )
    rates = jnp.stack([p[3] for p in prepared])
    skips = jnp.stack([d_skip[k] for k in ks])
    per = ordered[0].shape[1] // len(ks)
    axis = "cols" if ks[0] < 2 else "rows"

    def rate_of(rates):
        return jnp.repeat(jnp.swapaxes(rates, 1, 2), per, axis=0)

    h_zero = jnp.zeros((ordered[0].shape[1], rates.shape[2], rates.shape[1]), jnp.float32)

    def local_scan(act_in, step_in, b_part, readout_piece, rate_in, skip_in):
        return run_scan(
            h_zero, act_in, step_in, b_part, readout_piece, rate_of(rate_in),
            jnp.repeat(skip_in, per, axis=0),
        )

    (out_local, h_local), local_back = jax.vjp(
        local_scan, ordered[0], ordered[1], ordered[2], ordered[3], rates, skips
    )
    decay_factors, decay_back = jax.vjp(
        lambda s, r: cumulative_decay(s, rate_of(r)), ordered[1], rates
    )
    sums = jnp.cumsum(ordered[1], axis=0)[-1]
    h_start = entering(sums, h_local, rate_of(rates), axis, [k % 2 == 1 for k in ks])

    def carried(decay_in, readout_piece):
        extra = jnp.einsum(
            "lsne,lsn->lse", decay_in * h_start, readout_piece, precision=EXACT_MATH_MODE
        )
        return (extra, decay_in[-1] * h_start)

    (extra, _), carry_back = jax.vjp(carried, decay_factors, ordered[3])
    return (
        parted(out_local + extra, ks),
        (local_back, decay_back, carry_back, decay_factors, ordered[3], sums, rate_of(rates)),
    )


def chain_backward(ks, memory, g_sum):
    local_back, decay_back, carry_back, decay_factors, readout_piece, sums, rate_lines = memory
    axis = "cols" if ks[0] < 2 else "rows"
    output_gradient = joined([g_sum] * len(ks), ks)
    partial_total = jnp.einsum(
        "dwq,dwy,dwyq->wyq",
        output_gradient,
        readout_piece,
        decay_factors,
        precision=EXACT_MATH_MODE,
    )
    g_last = entering(sums, partial_total, rate_lines, axis, [k % 2 == 0 for k in ks])
    g_local = local_back((output_gradient, g_last))
    g_decay, g_c_carry = carry_back((output_gradient, g_last))
    g_step_carry, g_rate_carry = decay_back(g_decay)
    g_rate = g_local[4] + g_rate_carry
    return [
        (u, s, b, c, g_rate[i], g_local[5][i])
        for i, (u, s, b, c) in enumerate(
            zip(
                parted(g_local[0], ks),
                parted(g_local[1] + g_step_carry, ks),
                parted(g_local[2], ks),
                parted(g_local[3] + g_c_carry, ks),
            )
        )
    ]


def summed_everywhere(flat, axes):
    for axis in axes:
        devices = lax.axis_size(axis)
        if devices & (devices - 1):
            flat = lax.psum(flat, axis)
            continue
        stride = 1
        while stride < devices:
            flat = flat + lax.ppermute(flat, axis, [(i, i ^ stride) for i in range(devices)])
            stride *= 2
    return flat


PAIRS = ((0, 1), (2, 3))


def body(
    image,
    w_in,
    conv_w,
    conv_b,
    w_x,
    w_dt,
    dt_bias,
    a_log,
    d_skip,
    ln_gain,
    ln_bias,
    w_out,
    cotangent,
):
    width = w_in.shape[0]
    pixels = image.reshape(image.shape[0], image.shape[1] // width, width)
    (inner_in, gate_in), in_back = jax.vjp(project_in, pixels, w_in)
    padded = extended(inner_in, (("rows", 0), ("cols", 1)), 1)

    def conv_weights(taps, offsets):
        return convolve(padded, taps, offsets)

    conv_out, conv_back = jax.vjp(conv_weights, conv_w, conv_b)
    activated, act_back = jax.vjp(activate, conv_out)
    prepared_all = []
    prep_backs = []
    for k in range(4):
        prepared, prep_back = jax.vjp(prepare, activated, w_x[k], w_dt[k], dt_bias[k], a_log[k])
        prepared_all.append(prepared)
        prep_backs.append(prep_back)
    summed = jnp.zeros_like(activated)
    memories = []
    for ks in PAIRS:
        outputs, memory = chain_forward(ks, activated, [prepared_all[k] for k in ks], d_skip)
        for piece in outputs:
            summed = summed + piece
        memories.append(memory)
    output, fin_back = jax.vjp(finish, summed, gate_in, ln_gain, ln_bias, w_out)
    g_sum, g_gate, g_gain, g_lnb, g_wout = fin_back(cotangent.reshape(output.shape))
    g_u = jnp.zeros_like(activated)
    per_k = [None] * 4
    for ks, memory in zip(PAIRS, memories):
        for k, gradients in zip(ks, chain_backward(ks, memory, g_sum)):
            g_u = g_u + gradients[0]
            per_k[k] = gradients[1:]
    g_wx, g_wdt, g_bias, g_alog, g_skip = ([], [], [], [], [])
    for k in range(4):
        g_step, g_b, g_c, g_rate, g_skip_k = per_k[k]
        g_prep = prep_backs[k]((g_step, g_b, g_c, g_rate))
        g_u = g_u + g_prep[0]
        g_wx.append(g_prep[1])
        g_wdt.append(g_prep[2])
        g_bias.append(g_prep[3])
        g_alog.append(g_prep[4])
        g_skip.append(g_skip_k)
    g_conv = act_back(g_u)[0]
    g_cw, g_cb = conv_back(g_conv)
    g_pad = extended(g_conv, (("rows", 0), ("cols", 1)), 1)
    height = g_conv.shape[0]
    breadth = g_conv.shape[1]
    g_inner = conv_w[0] * g_pad[2 : 2 + height, 2 : 2 + breadth]
    for tap in range(1, 9):
        row_off = 2 - tap // 3
        col_off = 2 - tap % 3
        g_inner = (
            g_inner + conv_w[tap] * g_pad[row_off : row_off + height, col_off : col_off + breadth]
        )
    g_x, g_win = in_back((g_inner, g_gate))
    pieces = (
        g_win,
        g_cw,
        g_cb,
        jnp.stack(g_wx),
        jnp.stack(g_wdt),
        jnp.stack(g_bias),
        jnp.stack(g_alog),
        jnp.stack(g_skip),
        g_gain,
        g_lnb,
        g_wout,
    )
    flat = summed_everywhere(jnp.concatenate([p.reshape(-1) for p in pieces]), ("cols", "rows"))
    totals = []
    offset = 0
    for p in pieces:
        totals.append(flat[offset : offset + p.size].reshape(p.shape))
        offset += p.size
    return (
        output.reshape(image.shape),
        g_x.reshape(image.shape),
        totals[0],
        totals[1],
        totals[2],
        totals[3],
        totals[4],
        totals[5],
        totals[6],
        totals[7],
        totals[8],
        totals[9],
        totals[10],
    )


def solution(mesh):
    in_specs = (
        P("rows", "cols"),
        P(),
        P(),
        P(),
        P(),
        P(),
        P(),
        P(),
        P(),
        P(),
        P(),
        P(),
        P("rows", "cols"),
    )
    out_specs = (
        P("rows", "cols"),
        P("rows", "cols"),
        P(),
        P(),
        P(),
        P(),
        P(),
        P(),
        P(),
        P(),
        P(),
        P(),
        P(),
    )
    return jax.shard_map(body, mesh=mesh, in_specs=in_specs, out_specs=out_specs, check_vma=False)
```

```python
import jax
import jax.numpy as jnp
from jax import lax
from jax.sharding import PartitionSpec as P

EXACT_MATH_MODE = lax.Precision.HIGHEST


def entering(part, axis, flips):
    count = lax.axis_size(axis)
    place = lax.axis_index(axis)
    gathered = lax.all_gather(jnp.stack(part), axis)
    per = part[0].shape[0] // len(flips)
    states = []
    for group, reverse in enumerate(flips):
        ahead = count - 1 - place if reverse else place
        piece = gathered[:, :, group * per : (group + 1) * per]
        state = (jnp.ones_like(piece[0, 0]), jnp.zeros_like(piece[0, 1]))
        for lap in range(count - 1):
            source = count - 1 - lap if reverse else lap
            fresh = combine(state, (piece[source, 0], piece[source, 1]))
            state = jax.tree.map(lambda n, o: jnp.where(lap < ahead, n, o), fresh, state)
        states.append(state[1])
    return jnp.concatenate(states, axis=0)


def extended(array, sides, width):
    for axis, dim in sides:
        devices, length = (lax.axis_size(axis), array.shape[dim])
        up = [(i, (i + 1) % devices) for i in range(devices - 1)]
        down = [(j, i) for i, j in up]
        last = lax.slice_in_dim(array, length - width, length, axis=dim)
        leading = lax.slice_in_dim(array, 0, width, axis=dim)
        before = lax.ppermute(last, axis, up)
        after = lax.ppermute(leading, axis, down)
        array = jnp.concatenate([before, array, after], axis=dim)
    return array


def project_in(pixels, w_in):
    mixed = jnp.einsum("rcd,de->rce", pixels.astype(jnp.float32), w_in, precision=EXACT_MATH_MODE)
    halfway = w_in.shape[1] // 2
    return (mixed[:, :, :halfway], mixed[:, :, halfway:])


def convolve(padded, conv_w, conv_b):
    height = padded.shape[0] - 2
    breadth = padded.shape[1] - 2
    running = conv_b + conv_w[0] * padded[0:height, 0:breadth]
    for tap in range(1, 9):
        running = (
            running
            + conv_w[tap] * padded[tap // 3 : tap // 3 + height, tap % 3 : tap % 3 + breadth]
        )
    return running


def activate(conv_out):
    return jax.nn.silu(conv_out)


def prepare(activated, w_proj, w_step, step_bias, log_rate):
    width_rank = w_step.shape[0]
    state_width = log_rate.shape[1]
    projected = jnp.einsum("rce,ef->rcf", activated, w_proj, precision=EXACT_MATH_MODE)
    step_size = jax.nn.softplus(
        jnp.einsum("rcq,qe->rce", projected[:, :, :width_rank], w_step, precision=EXACT_MATH_MODE)
        + step_bias
    )
    b_in = projected[:, :, width_rank : width_rank + state_width]
    c_out = projected[:, :, width_rank + state_width :]
    return (step_size, b_in, c_out, -jnp.exp(log_rate))


def run_scan(h_start, activated, step_size, b_in, c_out, rate_lines, skip_lines):
    def advance(hidden_state, inputs):
        input_at_step, d_t, b_t, readout_at_step = inputs
        factor = jnp.exp(d_t[:, None, :] * rate_lines)
        hidden_state = factor * hidden_state + (d_t * input_at_step)[:, None, :] * b_t[:, :, None]
        final_answer = (
            jnp.sum(hidden_state * readout_at_step[:, :, None], axis=1)
            + skip_lines * input_at_step
        )
        return (hidden_state, final_answer)

    h_last, outputs = lax.scan(advance, h_start, (activated, step_size, b_in, c_out), unroll=8)
    return (outputs, h_last)


def cumulative_decay(step_size, rate_lines):
    return jnp.exp(jnp.cumsum(step_size, axis=0)[:, :, None, :] * rate_lines[None])


def arrange(values, k):
    if k < 2:
        values = jnp.swapaxes(values, 0, 1)
    if k % 2 == 1:
        values = jnp.flip(values, 0)
    return values


def restore(values, k):
    if k % 2 == 1:
        values = jnp.flip(values, 0)
    if k < 2:
        values = jnp.swapaxes(values, 0, 1)
    return values


def finish(summed, gate_in, ln_gain, ln_bias, w_out):
    average = jnp.mean(summed, axis=2, keepdims=True)
    centred = summed - average
    spread = jnp.mean(centred * centred, axis=2, keepdims=True)
    normed = centred * lax.rsqrt(spread + 1e-05) * ln_gain + ln_bias
    gated = normed * jax.nn.silu(gate_in)
    return jnp.einsum("rce,ed->rcd", gated, w_out, precision=EXACT_MATH_MODE).astype(jnp.bfloat16)


def combine(earlier, later):
    return (earlier[0] * later[0], later[1] + later[0] * earlier[1])


def joined(values, ks):
    return jnp.concatenate([arrange(v, k) for v, k in zip(values, ks)], axis=1)


def parted(values, ks):
    return [restore(v, k) for v, k in zip(jnp.split(values, len(ks), axis=1), ks)]


def chain_forward(ks, activated, prepared, d_skip):
    ordered = (
        joined([activated] * len(ks), ks),
        joined([p[0] for p in prepared], ks),
        joined([p[1] for p in prepared], ks),
        joined([p[2] for p in prepared], ks),
    )
    rates = jnp.stack([p[3] for p in prepared])
    skips = jnp.stack([d_skip[k] for k in ks])
    per = ordered[0].shape[1] // len(ks)
    axis = "cols" if ks[0] < 2 else "rows"

    def rate_of(rates):
        return jnp.repeat(jnp.swapaxes(rates, 1, 2), per, axis=0)

    h_zero = jnp.zeros((ordered[0].shape[1], rates.shape[2], rates.shape[1]), jnp.float32)

    def local_scan(act_in, step_in, b_part, readout_piece, rate_in, skip_in):
        return run_scan(
            h_zero, act_in, step_in, b_part, readout_piece, rate_of(rate_in),
            jnp.repeat(skip_in, per, axis=0),
        )

    (out_local, h_local), local_back = jax.vjp(
        local_scan, ordered[0], ordered[1], ordered[2], ordered[3], rates, skips
    )
    decay_factors, decay_back = jax.vjp(
        lambda s, r: cumulative_decay(s, rate_of(r)), ordered[1], rates
    )
    fading = decay_factors[-1]
    h_start = entering((fading, h_local), axis, [k % 2 == 1 for k in ks])

    def carried(decay_in, readout_piece):
        extra = jnp.sum(decay_in * h_start * readout_piece[:, :, :, None], axis=2)
        return (extra, decay_in[-1] * h_start)

    (extra, _), carry_back = jax.vjp(carried, decay_factors, ordered[3])
    return (
        parted(out_local + extra, ks),
        (local_back, decay_back, carry_back, decay_factors, ordered[3]),
    )


def chain_backward(ks, memory, g_sum):
    local_back, decay_back, carry_back, decay_factors, readout_piece = memory
    axis = "cols" if ks[0] < 2 else "rows"
    output_gradient = joined([g_sum] * len(ks), ks)
    partial_total = jnp.sum(
        output_gradient[:, :, None, :] * readout_piece[:, :, :, None] * decay_factors, axis=0
    )
    g_last = entering((decay_factors[-1], partial_total), axis, [k % 2 == 0 for k in ks])
    g_local = local_back((output_gradient, g_last))
    g_decay, g_c_carry = carry_back((output_gradient, g_last))
    g_step_carry, g_rate_carry = decay_back(g_decay)
    g_rate = g_local[4] + g_rate_carry
    return [
        (u, s, b, c, g_rate[i], g_local[5][i])
        for i, (u, s, b, c) in enumerate(
            zip(
                parted(g_local[0], ks),
                parted(g_local[1] + g_step_carry, ks),
                parted(g_local[2], ks),
                parted(g_local[3] + g_c_carry, ks),
            )
        )
    ]


def summed_everywhere(flat, axes):
    for axis in axes:
        devices = lax.axis_size(axis)
        if devices & (devices - 1):
            flat = lax.psum(flat, axis)
            continue
        stride = 1
        while stride < devices:
            flat = flat + lax.ppermute(flat, axis, [(i, i ^ stride) for i in range(devices)])
            stride *= 2
    return flat


PAIRS = ((0, 1), (2, 3))


def body(
    image,
    w_in,
    conv_w,
    conv_b,
    w_x,
    w_dt,
    dt_bias,
    a_log,
    d_skip,
    ln_gain,
    ln_bias,
    w_out,
    cotangent,
):
    width = w_in.shape[0]
    pixels = image.reshape(image.shape[0], image.shape[1] // width, width)
    (inner_in, gate_in), in_back = jax.vjp(project_in, pixels, w_in)
    padded = extended(inner_in, (("rows", 0), ("cols", 1)), 1)

    def conv_weights(taps, offsets):
        return convolve(padded, taps, offsets)

    conv_out, conv_back = jax.vjp(conv_weights, conv_w, conv_b)
    activated, act_back = jax.vjp(activate, conv_out)
    prepared_all = []
    prep_backs = []
    for k in range(4):
        prepared, prep_back = jax.vjp(prepare, activated, w_x[k], w_dt[k], dt_bias[k], a_log[k])
        prepared_all.append(prepared)
        prep_backs.append(prep_back)
    summed = jnp.zeros_like(activated)
    memories = []
    for ks in PAIRS:
        outputs, memory = chain_forward(ks, activated, [prepared_all[k] for k in ks], d_skip)
        for piece in outputs:
            summed = summed + piece
        memories.append(memory)
    output, fin_back = jax.vjp(finish, summed, gate_in, ln_gain, ln_bias, w_out)
    g_sum, g_gate, g_gain, g_lnb, g_wout = fin_back(cotangent.reshape(output.shape))
    g_u = jnp.zeros_like(activated)
    per_k = [None] * 4
    for ks, memory in zip(PAIRS, memories):
        for k, gradients in zip(ks, chain_backward(ks, memory, g_sum)):
            g_u = g_u + gradients[0]
            per_k[k] = gradients[1:]
    g_wx, g_wdt, g_bias, g_alog, g_skip = ([], [], [], [], [])
    for k in range(4):
        g_step, g_b, g_c, g_rate, g_skip_k = per_k[k]
        g_prep = prep_backs[k]((g_step, g_b, g_c, g_rate))
        g_u = g_u + g_prep[0]
        g_wx.append(g_prep[1])
        g_wdt.append(g_prep[2])
        g_bias.append(g_prep[3])
        g_alog.append(g_prep[4])
        g_skip.append(g_skip_k)
    g_conv = act_back(g_u)[0]
    g_cw, g_cb = conv_back(g_conv)
    g_pad = extended(g_conv, (("rows", 0), ("cols", 1)), 1)
    height = g_conv.shape[0]
    breadth = g_conv.shape[1]
    g_inner = conv_w[0] * g_pad[2 : 2 + height, 2 : 2 + breadth]
    for tap in range(1, 9):
        row_off = 2 - tap // 3
        col_off = 2 - tap % 3
        g_inner = (
            g_inner + conv_w[tap] * g_pad[row_off : row_off + height, col_off : col_off + breadth]
        )
    g_x, g_win = in_back((g_inner, g_gate))
    pieces = (
        g_win,
        g_cw,
        g_cb,
        jnp.stack(g_wx),
        jnp.stack(g_wdt),
        jnp.stack(g_bias),
        jnp.stack(g_alog),
        jnp.stack(g_skip),
        g_gain,
        g_lnb,
        g_wout,
    )
    flat = summed_everywhere(jnp.concatenate([p.reshape(-1) for p in pieces]), ("cols", "rows"))
    totals = []
    offset = 0
    for p in pieces:
        totals.append(flat[offset : offset + p.size].reshape(p.shape))
        offset += p.size
    return (
        output.reshape(image.shape),
        g_x.reshape(image.shape),
        totals[0],
        totals[1],
        totals[2],
        totals[3],
        totals[4],
        totals[5],
        totals[6],
        totals[7],
        totals[8],
        totals[9],
        totals[10],
    )


def solution(mesh):
    in_specs = (
        P("rows", "cols"),
        P(),
        P(),
        P(),
        P(),
        P(),
        P(),
        P(),
        P(),
        P(),
        P(),
        P(),
        P("rows", "cols"),
    )
    out_specs = (
        P("rows", "cols"),
        P("rows", "cols"),
        P(),
        P(),
        P(),
        P(),
        P(),
        P(),
        P(),
        P(),
        P(),
        P(),
        P(),
    )
    return jax.shard_map(body, mesh=mesh, in_specs=in_specs, out_specs=out_specs, check_vma=False)
```

```python
import jax
import jax.numpy as jnp
from jax import lax
from jax.sharding import PartitionSpec as P

EXACT_MATH_MODE = lax.Precision.HIGHEST


def entering(sums, part, rate_lines, axis, flips):
    count = lax.axis_size(axis)
    place = lax.axis_index(axis)
    gathered = lax.all_gather(jnp.concatenate([sums[:, None, :], part], axis=1), axis)
    per = part.shape[0] // len(flips)
    states = []
    for group, reverse in enumerate(flips):
        ahead = count - 1 - place if reverse else place
        piece = gathered[:, group * per : (group + 1) * per]
        rate = rate_lines[group * per : (group + 1) * per]
        state = (jnp.ones_like(piece[0, :, 1:]), jnp.zeros_like(piece[0, :, 1:]))
        for lap in range(count - 1):
            source = count - 1 - lap if reverse else lap
            fading = jnp.exp(piece[source, :, :1] * rate)
            fresh = combine(state, (fading, piece[source, :, 1:]))
            state = jax.tree.map(lambda n, o: jnp.where(lap < ahead, n, o), fresh, state)
        states.append(state[1])
    return jnp.concatenate(states, axis=0)


def extended(array, sides, width):
    for axis, dim in sides:
        devices, length = (lax.axis_size(axis), array.shape[dim])
        up = [(i, (i + 1) % devices) for i in range(devices - 1)]
        down = [(j, i) for i, j in up]
        last = lax.slice_in_dim(array, length - width, length, axis=dim)
        leading = lax.slice_in_dim(array, 0, width, axis=dim)
        before = lax.ppermute(last, axis, up)
        after = lax.ppermute(leading, axis, down)
        array = jnp.concatenate([before, array, after], axis=dim)
    return array


def project_in(pixels, w_in):
    mixed = jnp.einsum("rcd,de->rce", pixels.astype(jnp.float32), w_in, precision=EXACT_MATH_MODE)
    halfway = w_in.shape[1] // 2
    return (mixed[:, :, :halfway], mixed[:, :, halfway:])


def convolve(padded, conv_w, conv_b):
    height = padded.shape[0] - 2
    breadth = padded.shape[1] - 2
    running = conv_b + conv_w[0] * padded[0:height, 0:breadth]
    for tap in range(1, 9):
        running = (
            running
            + conv_w[tap] * padded[tap // 3 : tap // 3 + height, tap % 3 : tap % 3 + breadth]
        )
    return running


def activate(conv_out):
    return jax.nn.silu(conv_out)


def prepare(activated, w_proj, w_step, step_bias, log_rate):
    width_rank = w_step.shape[0]
    state_width = log_rate.shape[1]
    projected = jnp.einsum("rce,ef->rcf", activated, w_proj, precision=EXACT_MATH_MODE)
    step_size = jax.nn.softplus(
        jnp.einsum("rcq,qe->rce", projected[:, :, :width_rank], w_step, precision=EXACT_MATH_MODE)
        + step_bias
    )
    b_in = projected[:, :, width_rank : width_rank + state_width]
    c_out = projected[:, :, width_rank + state_width :]
    return (step_size, b_in, c_out, -jnp.exp(log_rate))


def run_scan(h_start, activated, step_size, b_in, c_out, rate_lines, skip_lines):
    def advance(hidden_state, inputs):
        input_at_step, d_t, b_t, readout_at_step = inputs
        factor = jnp.exp(d_t[:, None, :] * rate_lines)
        hidden_state = factor * hidden_state + (d_t * input_at_step)[:, None, :] * b_t[:, :, None]
        final_answer = (
            jnp.sum(hidden_state * readout_at_step[:, :, None], axis=1)
            + skip_lines * input_at_step
        )
        return (hidden_state, final_answer)

    h_last, outputs = lax.scan(advance, h_start, (activated, step_size, b_in, c_out), unroll=8)
    return (outputs, h_last)


def cumulative_decay(step_size, rate_lines):
    return jnp.exp(jnp.cumsum(step_size, axis=0)[:, :, None, :] * rate_lines[None])


def arrange(values, k):
    if k < 2:
        values = jnp.swapaxes(values, 0, 1)
    if k % 2 == 1:
        values = jnp.flip(values, 0)
    return values


def restore(values, k):
    if k % 2 == 1:
        values = jnp.flip(values, 0)
    if k < 2:
        values = jnp.swapaxes(values, 0, 1)
    return values


def finish(summed, gate_in, ln_gain, ln_bias, w_out):
    average = jnp.mean(summed, axis=2, keepdims=True)
    centred = summed - average
    spread = jnp.mean(centred * centred, axis=2, keepdims=True)
    normed = centred * lax.rsqrt(spread + 1e-05) * ln_gain + ln_bias
    gated = normed * jax.nn.silu(gate_in)
    return jnp.einsum("rce,ed->rcd", gated, w_out, precision=EXACT_MATH_MODE).astype(jnp.bfloat16)


def combine(earlier, later):
    return (earlier[0] * later[0], later[1] + later[0] * earlier[1])


def joined(values, ks):
    return jnp.concatenate([arrange(v, k) for v, k in zip(values, ks)], axis=1)


def parted(values, ks):
    return [restore(v, k) for v, k in zip(jnp.split(values, len(ks), axis=1), ks)]


def chain_forward(ks, activated, prepared, d_skip):
    ordered = (
        joined([activated] * len(ks), ks),
        joined([p[0] for p in prepared], ks),
        joined([p[1] for p in prepared], ks),
        joined([p[2] for p in prepared], ks),
    )
    rates = jnp.stack([p[3] for p in prepared])
    skips = jnp.stack([d_skip[k] for k in ks])
    per = ordered[0].shape[1] // len(ks)
    axis = "cols" if ks[0] < 2 else "rows"

    def rate_of(rates):
        return jnp.repeat(jnp.swapaxes(rates, 1, 2), per, axis=0)

    h_zero = jnp.zeros((ordered[0].shape[1], rates.shape[2], rates.shape[1]), jnp.float32)

    def local_scan(act_in, step_in, b_part, readout_piece, rate_in, skip_in):
        return run_scan(
            h_zero, act_in, step_in, b_part, readout_piece, rate_of(rate_in),
            jnp.repeat(skip_in, per, axis=0),
        )

    (out_local, h_local), local_back = jax.vjp(
        local_scan, ordered[0], ordered[1], ordered[2], ordered[3], rates, skips
    )
    decay_factors, decay_back = jax.vjp(
        lambda s, r: cumulative_decay(s, rate_of(r)), ordered[1], rates
    )
    sums = jnp.cumsum(ordered[1], axis=0)[-1]
    h_start = entering(sums, h_local, rate_of(rates), axis, [k % 2 == 1 for k in ks])

    def carried(decay_in, readout_piece):
        extra = jnp.sum(decay_in * h_start * readout_piece[:, :, :, None], axis=2)
        return (extra, decay_in[-1] * h_start)

    (extra, _), carry_back = jax.vjp(carried, decay_factors, ordered[3])
    return (
        parted(out_local + extra, ks),
        (local_back, decay_back, carry_back, decay_factors, ordered[3], sums, rate_of(rates)),
    )


def chain_backward(ks, memory, g_sum):
    local_back, decay_back, carry_back, decay_factors, readout_piece, sums, rate_lines = memory
    axis = "cols" if ks[0] < 2 else "rows"
    output_gradient = joined([g_sum] * len(ks), ks)
    partial_total = jnp.sum(
        output_gradient[:, :, None, :] * readout_piece[:, :, :, None] * decay_factors, axis=0
    )
    g_last = entering(sums, partial_total, rate_lines, axis, [k % 2 == 0 for k in ks])
    g_local = local_back((output_gradient, g_last))
    g_decay, g_c_carry = carry_back((output_gradient, g_last))
    g_step_carry, g_rate_carry = decay_back(g_decay)
    g_rate = g_local[4] + g_rate_carry
    return [
        (u, s, b, c, g_rate[i], g_local[5][i])
        for i, (u, s, b, c) in enumerate(
            zip(
                parted(g_local[0], ks),
                parted(g_local[1] + g_step_carry, ks),
                parted(g_local[2], ks),
                parted(g_local[3] + g_c_carry, ks),
            )
        )
    ]


def summed_everywhere(flat, axes):
    for axis in axes:
        devices = lax.axis_size(axis)
        if devices & (devices - 1):
            flat = lax.psum(flat, axis)
            continue
        stride = 1
        while stride < devices:
            flat = flat + lax.ppermute(flat, axis, [(i, i ^ stride) for i in range(devices)])
            stride *= 2
    return flat


PAIRS = ((0, 1), (2, 3))


def body(
    image,
    w_in,
    conv_w,
    conv_b,
    w_x,
    w_dt,
    dt_bias,
    a_log,
    d_skip,
    ln_gain,
    ln_bias,
    w_out,
    cotangent,
):
    width = w_in.shape[0]
    pixels = image.reshape(image.shape[0], image.shape[1] // width, width)
    (inner_in, gate_in), in_back = jax.vjp(project_in, pixels, w_in)
    padded = extended(inner_in, (("rows", 0), ("cols", 1)), 1)

    def conv_weights(taps, offsets):
        return convolve(padded, taps, offsets)

    conv_out, conv_back = jax.vjp(conv_weights, conv_w, conv_b)
    activated, act_back = jax.vjp(activate, conv_out)
    prepared_all = []
    prep_backs = []
    for k in range(4):
        prepared, prep_back = jax.vjp(prepare, activated, w_x[k], w_dt[k], dt_bias[k], a_log[k])
        prepared_all.append(prepared)
        prep_backs.append(prep_back)
    summed = jnp.zeros_like(activated)
    memories = []
    for ks in PAIRS:
        outputs, memory = chain_forward(ks, activated, [prepared_all[k] for k in ks], d_skip)
        for piece in outputs:
            summed = summed + piece
        memories.append(memory)
    output, fin_back = jax.vjp(finish, summed, gate_in, ln_gain, ln_bias, w_out)
    g_sum, g_gate, g_gain, g_lnb, g_wout = fin_back(cotangent.reshape(output.shape))
    g_u = jnp.zeros_like(activated)
    per_k = [None] * 4
    for ks, memory in zip(PAIRS, memories):
        for k, gradients in zip(ks, chain_backward(ks, memory, g_sum)):
            g_u = g_u + gradients[0]
            per_k[k] = gradients[1:]
    g_wx, g_wdt, g_bias, g_alog, g_skip = ([], [], [], [], [])
    for k in range(4):
        g_step, g_b, g_c, g_rate, g_skip_k = per_k[k]
        g_prep = prep_backs[k]((g_step, g_b, g_c, g_rate))
        g_u = g_u + g_prep[0]
        g_wx.append(g_prep[1])
        g_wdt.append(g_prep[2])
        g_bias.append(g_prep[3])
        g_alog.append(g_prep[4])
        g_skip.append(g_skip_k)
    g_conv = act_back(g_u)[0]
    g_cw, g_cb = conv_back(g_conv)
    g_pad = extended(g_conv, (("rows", 0), ("cols", 1)), 1)
    height = g_conv.shape[0]
    breadth = g_conv.shape[1]
    g_inner = conv_w[0] * g_pad[2 : 2 + height, 2 : 2 + breadth]
    for tap in range(1, 9):
        row_off = 2 - tap // 3
        col_off = 2 - tap % 3
        g_inner = (
            g_inner + conv_w[tap] * g_pad[row_off : row_off + height, col_off : col_off + breadth]
        )
    g_x, g_win = in_back((g_inner, g_gate))
    pieces = (
        g_win,
        g_cw,
        g_cb,
        jnp.stack(g_wx),
        jnp.stack(g_wdt),
        jnp.stack(g_bias),
        jnp.stack(g_alog),
        jnp.stack(g_skip),
        g_gain,
        g_lnb,
        g_wout,
    )
    flat = summed_everywhere(jnp.concatenate([p.reshape(-1) for p in pieces]), ("cols", "rows"))
    totals = []
    offset = 0
    for p in pieces:
        totals.append(flat[offset : offset + p.size].reshape(p.shape))
        offset += p.size
    return (
        output.reshape(image.shape),
        g_x.reshape(image.shape),
        totals[0],
        totals[1],
        totals[2],
        totals[3],
        totals[4],
        totals[5],
        totals[6],
        totals[7],
        totals[8],
        totals[9],
        totals[10],
    )


def solution(mesh):
    in_specs = (
        P("rows", "cols"),
        P(),
        P(),
        P(),
        P(),
        P(),
        P(),
        P(),
        P(),
        P(),
        P(),
        P(),
        P("rows", "cols"),
    )
    out_specs = (
        P("rows", "cols"),
        P("rows", "cols"),
        P(),
        P(),
        P(),
        P(),
        P(),
        P(),
        P(),
        P(),
        P(),
        P(),
        P(),
    )
    return jax.shard_map(body, mesh=mesh, in_specs=in_specs, out_specs=out_specs, check_vma=False)
```

```python
import jax
import jax.numpy as jnp
from jax import lax
from jax.sharding import PartitionSpec as P

EXACT_MATH_MODE = lax.Precision.HIGHEST


def entering(part, axis, flips):
    count = lax.axis_size(axis)
    place = lax.axis_index(axis)
    gathered = lax.all_gather(jnp.stack(part), axis)
    per = part[0].shape[0] // len(flips)
    states = []
    for group, reverse in enumerate(flips):
        ahead = count - 1 - place if reverse else place
        piece = gathered[:, :, group * per : (group + 1) * per]
        state = (jnp.ones_like(piece[0, 0]), jnp.zeros_like(piece[0, 1]))
        for lap in range(count - 1):
            source = count - 1 - lap if reverse else lap
            fresh = combine(state, (piece[source, 0], piece[source, 1]))
            state = jax.tree.map(lambda n, o: jnp.where(lap < ahead, n, o), fresh, state)
        states.append(state[1])
    return jnp.concatenate(states, axis=0)


def extended(array, sides, width):
    for axis, dim in sides:
        devices, length = (lax.axis_size(axis), array.shape[dim])
        up = [(i, (i + 1) % devices) for i in range(devices - 1)]
        down = [(j, i) for i, j in up]
        last = lax.slice_in_dim(array, length - width, length, axis=dim)
        leading = lax.slice_in_dim(array, 0, width, axis=dim)
        before = lax.ppermute(last, axis, up)
        after = lax.ppermute(leading, axis, down)
        array = jnp.concatenate([before, array, after], axis=dim)
    return array


def project_in(pixels, w_in):
    mixed = jnp.einsum("rcd,de->rce", pixels.astype(jnp.float32), w_in, precision=EXACT_MATH_MODE)
    halfway = w_in.shape[1] // 2
    return (mixed[:, :, :halfway], mixed[:, :, halfway:])


def convolve(padded, conv_w, conv_b):
    height = padded.shape[0] - 2
    breadth = padded.shape[1] - 2
    running = conv_b + conv_w[0] * padded[0:height, 0:breadth]
    for tap in range(1, 9):
        running = (
            running
            + conv_w[tap] * padded[tap // 3 : tap // 3 + height, tap % 3 : tap % 3 + breadth]
        )
    return running


def activate(conv_out):
    return jax.nn.silu(conv_out)


def prepare(activated, w_proj, w_step, step_bias, log_rate):
    width_rank = w_step.shape[0]
    state_width = log_rate.shape[1]
    projected = jnp.einsum("rce,ef->rcf", activated, w_proj, precision=EXACT_MATH_MODE)
    low_rank = projected[:, :, 0:1] * w_step[0]
    for q in range(1, width_rank):
        low_rank = low_rank + projected[:, :, q : q + 1] * w_step[q]
    step_size = jax.nn.softplus(low_rank + step_bias)
    b_in = projected[:, :, width_rank : width_rank + state_width]
    c_out = projected[:, :, width_rank + state_width :]
    return (step_size, b_in, c_out, -jnp.exp(log_rate))


def run_scan(h_start, activated, step_size, b_in, c_out, rate_lines, skip_lines):
    def advance(hidden_state, inputs):
        input_at_step, d_t, b_t, readout_at_step = inputs
        factor = jnp.exp(d_t[:, None, :] * rate_lines)
        hidden_state = factor * hidden_state + (d_t * input_at_step)[:, None, :] * b_t[:, :, None]
        final_answer = (
            jnp.sum(hidden_state * readout_at_step[:, :, None], axis=1)
            + skip_lines * input_at_step
        )
        return (hidden_state, final_answer)

    h_last, outputs = lax.scan(advance, h_start, (activated, step_size, b_in, c_out), unroll=8)
    return (outputs, h_last)


def cumulative_decay(step_size, rate_lines):
    return jnp.exp(jnp.cumsum(step_size, axis=0)[:, :, None, :] * rate_lines[None])


def arrange(values, k):
    if k < 2:
        values = jnp.swapaxes(values, 0, 1)
    if k % 2 == 1:
        values = jnp.flip(values, 0)
    return values


def restore(values, k):
    if k % 2 == 1:
        values = jnp.flip(values, 0)
    if k < 2:
        values = jnp.swapaxes(values, 0, 1)
    return values


def finish(summed, gate_in, ln_gain, ln_bias, w_out):
    average = jnp.mean(summed, axis=2, keepdims=True)
    centred = summed - average
    spread = jnp.mean(centred * centred, axis=2, keepdims=True)
    normed = centred * lax.rsqrt(spread + 1e-05) * ln_gain + ln_bias
    gated = normed * jax.nn.silu(gate_in)
    return jnp.einsum("rce,ed->rcd", gated, w_out, precision=EXACT_MATH_MODE).astype(jnp.bfloat16)


def combine(earlier, later):
    return (earlier[0] * later[0], later[1] + later[0] * earlier[1])


def joined(values, ks):
    return jnp.concatenate([arrange(v, k) for v, k in zip(values, ks)], axis=1)


def parted(values, ks):
    return [restore(v, k) for v, k in zip(jnp.split(values, len(ks), axis=1), ks)]


def chain_forward(ks, activated, prepared, d_skip):
    ordered = (
        joined([activated] * len(ks), ks),
        joined([p[0] for p in prepared], ks),
        joined([p[1] for p in prepared], ks),
        joined([p[2] for p in prepared], ks),
    )
    rates = jnp.stack([p[3] for p in prepared])
    skips = jnp.stack([d_skip[k] for k in ks])
    per = ordered[0].shape[1] // len(ks)
    axis = "cols" if ks[0] < 2 else "rows"

    def rate_of(rates):
        return jnp.repeat(jnp.swapaxes(rates, 1, 2), per, axis=0)

    h_zero = jnp.zeros((ordered[0].shape[1], rates.shape[2], rates.shape[1]), jnp.float32)

    def local_scan(act_in, step_in, b_part, readout_piece, rate_in, skip_in):
        return run_scan(
            h_zero, act_in, step_in, b_part, readout_piece, rate_of(rate_in),
            jnp.repeat(skip_in, per, axis=0),
        )

    (out_local, h_local), local_back = jax.vjp(
        local_scan, ordered[0], ordered[1], ordered[2], ordered[3], rates, skips
    )
    decay_factors, decay_back = jax.vjp(
        lambda s, r: cumulative_decay(s, rate_of(r)), ordered[1], rates
    )
    fading = decay_factors[-1]
    h_start = entering((fading, h_local), axis, [k % 2 == 1 for k in ks])

    def carried(decay_in, readout_piece):
        extra = jnp.sum(decay_in * h_start * readout_piece[:, :, :, None], axis=2)
        return (extra, decay_in[-1] * h_start)

    (extra, _), carry_back = jax.vjp(carried, decay_factors, ordered[3])
    return (
        parted(out_local + extra, ks),
        (local_back, decay_back, carry_back, decay_factors, ordered[3]),
    )


def chain_backward(ks, memory, g_sum):
    local_back, decay_back, carry_back, decay_factors, readout_piece = memory
    axis = "cols" if ks[0] < 2 else "rows"
    output_gradient = joined([g_sum] * len(ks), ks)
    partial_total = jnp.sum(
        output_gradient[:, :, None, :] * readout_piece[:, :, :, None] * decay_factors, axis=0
    )
    g_last = entering((decay_factors[-1], partial_total), axis, [k % 2 == 0 for k in ks])
    g_local = local_back((output_gradient, g_last))
    g_decay, g_c_carry = carry_back((output_gradient, g_last))
    g_step_carry, g_rate_carry = decay_back(g_decay)
    g_rate = g_local[4] + g_rate_carry
    return [
        (u, s, b, c, g_rate[i], g_local[5][i])
        for i, (u, s, b, c) in enumerate(
            zip(
                parted(g_local[0], ks),
                parted(g_local[1] + g_step_carry, ks),
                parted(g_local[2], ks),
                parted(g_local[3] + g_c_carry, ks),
            )
        )
    ]


def summed_everywhere(flat, axes):
    for axis in axes:
        devices = lax.axis_size(axis)
        if devices & (devices - 1):
            flat = lax.psum(flat, axis)
            continue
        stride = 1
        while stride < devices:
            flat = flat + lax.ppermute(flat, axis, [(i, i ^ stride) for i in range(devices)])
            stride *= 2
    return flat


PAIRS = ((0, 1), (2, 3))


def body(
    image,
    w_in,
    conv_w,
    conv_b,
    w_x,
    w_dt,
    dt_bias,
    a_log,
    d_skip,
    ln_gain,
    ln_bias,
    w_out,
    cotangent,
):
    width = w_in.shape[0]
    pixels = image.reshape(image.shape[0], image.shape[1] // width, width)
    (inner_in, gate_in), in_back = jax.vjp(project_in, pixels, w_in)
    padded = extended(inner_in, (("rows", 0), ("cols", 1)), 1)

    def conv_weights(taps, offsets):
        return convolve(padded, taps, offsets)

    conv_out, conv_back = jax.vjp(conv_weights, conv_w, conv_b)
    activated, act_back = jax.vjp(activate, conv_out)
    prepared_all = []
    prep_backs = []
    for k in range(4):
        prepared, prep_back = jax.vjp(prepare, activated, w_x[k], w_dt[k], dt_bias[k], a_log[k])
        prepared_all.append(prepared)
        prep_backs.append(prep_back)
    summed = jnp.zeros_like(activated)
    memories = []
    for ks in PAIRS:
        outputs, memory = chain_forward(ks, activated, [prepared_all[k] for k in ks], d_skip)
        for piece in outputs:
            summed = summed + piece
        memories.append(memory)
    output, fin_back = jax.vjp(finish, summed, gate_in, ln_gain, ln_bias, w_out)
    g_sum, g_gate, g_gain, g_lnb, g_wout = fin_back(cotangent.reshape(output.shape))
    g_u = jnp.zeros_like(activated)
    per_k = [None] * 4
    for ks, memory in zip(PAIRS, memories):
        for k, gradients in zip(ks, chain_backward(ks, memory, g_sum)):
            g_u = g_u + gradients[0]
            per_k[k] = gradients[1:]
    g_wx, g_wdt, g_bias, g_alog, g_skip = ([], [], [], [], [])
    for k in range(4):
        g_step, g_b, g_c, g_rate, g_skip_k = per_k[k]
        g_prep = prep_backs[k]((g_step, g_b, g_c, g_rate))
        g_u = g_u + g_prep[0]
        g_wx.append(g_prep[1])
        g_wdt.append(g_prep[2])
        g_bias.append(g_prep[3])
        g_alog.append(g_prep[4])
        g_skip.append(g_skip_k)
    g_conv = act_back(g_u)[0]
    g_cw, g_cb = conv_back(g_conv)
    g_pad = extended(g_conv, (("rows", 0), ("cols", 1)), 1)
    height = g_conv.shape[0]
    breadth = g_conv.shape[1]
    g_inner = conv_w[0] * g_pad[2 : 2 + height, 2 : 2 + breadth]
    for tap in range(1, 9):
        row_off = 2 - tap // 3
        col_off = 2 - tap % 3
        g_inner = (
            g_inner + conv_w[tap] * g_pad[row_off : row_off + height, col_off : col_off + breadth]
        )
    g_x, g_win = in_back((g_inner, g_gate))
    pieces = (
        g_win,
        g_cw,
        g_cb,
        jnp.stack(g_wx),
        jnp.stack(g_wdt),
        jnp.stack(g_bias),
        jnp.stack(g_alog),
        jnp.stack(g_skip),
        g_gain,
        g_lnb,
        g_wout,
    )
    flat = summed_everywhere(jnp.concatenate([p.reshape(-1) for p in pieces]), ("cols", "rows"))
    totals = []
    offset = 0
    for p in pieces:
        totals.append(flat[offset : offset + p.size].reshape(p.shape))
        offset += p.size
    return (
        output.reshape(image.shape),
        g_x.reshape(image.shape),
        totals[0],
        totals[1],
        totals[2],
        totals[3],
        totals[4],
        totals[5],
        totals[6],
        totals[7],
        totals[8],
        totals[9],
        totals[10],
    )


def solution(mesh):
    in_specs = (
        P("rows", "cols"),
        P(),
        P(),
        P(),
        P(),
        P(),
        P(),
        P(),
        P(),
        P(),
        P(),
        P(),
        P("rows", "cols"),
    )
    out_specs = (
        P("rows", "cols"),
        P("rows", "cols"),
        P(),
        P(),
        P(),
        P(),
        P(),
        P(),
        P(),
        P(),
        P(),
        P(),
        P(),
    )
    return jax.shard_map(body, mesh=mesh, in_specs=in_specs, out_specs=out_specs, check_vma=False)
```
